32 devices in a mesh: orb: 4 (over y, x), grid: 8 (over z, core).
Axes of the slice: x: 2, y: 2, z: 4, core: 2. Of those that a mesh axis runs over, the one named last changes fastest.
Arguments:
- orbitals: float32 [4, 96, 192, 256], P('orb', 'grid'), may hold values from -6 to 6
- potential: float32 [96, 192, 256], P('grid'), may hold values from -4 to 0
- trial_potential: float32 [96, 192, 256], P('grid'), may hold values from -6 to 6
- eigenvalues: float32 [4], P('orb'), may hold values from -3 to 0
- frequency: float32 [1], replicated, may hold values from 1 to 8
Outputs:
- solutions: float32 [4, 96, 192, 256], P('orb', 'grid')
- density: float32 [96, 192, 256], P('grid', 'orb')
The draws below stay inside these ranges and needn't reach their ends.
All inputs are finite; a program needn't handle non-finite values.
Results may differ from the reference program's by a relative error of at most 0.0001.
Values sent between devices are 32-bit elements; how exact they have to be, the bound alone decides.
A program may use at most 192 MiB of HBM per device.

```python
import math
import jax
import jax.numpy as jnp
from jax import lax

NY = 192
NZ = 256
ITERS = 2
NORB = 4
NX = 96


def level_of(stream_key, dims, cuts, low, top_value):
    factor_of = 1.0
    for position, blocks in cuts:
        heights = jax.random.uniform(jax.random.fold_in(jax.random.fold_in(stream_key, 6), position), (blocks,), jnp.float32, low / len(cuts), top_value / len(cuts))
        factor_of = factor_of * jnp.repeat(jnp.exp(heights), dims[position] // blocks).reshape((-1,) + (1,) * (len(dims) - 1 - position))
    return factor_of


def gaussian(own_key, shape, scale, most, split=(), kind=jnp.bfloat16):
    array = jax.random.normal(own_key, shape, jnp.float32) * scale
    if len(split) > 0:
        array = level_of(own_key, shape, split, -0.22, 0.18) * array
    return jnp.clip(array, min=-most, max=most).astype(kind)


def setup_inputs(seed: int = 0) -> dict:
    key_list = jax.random.split(jax.random.key(seed), 6)
    return {
        "orbitals": gaussian(key_list[0], (NORB, NX, NY, NZ), 1.0, 6.0, ((0, 4), (1, 8)), jnp.float32),
        "potential": jnp.clip(-4.0 + 4.0 * jax.random.uniform(key_list[1], (NX, NY, NZ), jnp.float32) ** level_of(key_list[1], (NX, NY, NZ), ((0, 8),), -0.2, 0.2), -4.0, 0.0),
        "trial_potential": gaussian(key_list[2], (NX, NY, NZ), 1.0, 6.0, ((0, 8),), jnp.float32),
        "eigenvalues": jnp.clip(-3.0 + 3.0 * jax.random.uniform(key_list[3], (NORB,), jnp.float32) ** level_of(key_list[3], (NORB,), ((0, 4),), -0.2, 0.2), -3.0, 0.0),
        "frequency": jnp.clip(jnp.exp(jax.random.uniform(key_list[4], (1,), jnp.float32, math.log(1.0), math.log(8.0))), 1.0, 8.0),
    }


STENCIL = (-5369.0 / 1800.0, 12.0 / 7.0, -15.0 / 56.0, 10.0 / 189.0, -1.0 / 112.0, 2.0 / 1925.0, -1.0 / 16632.0)
SPACING = 0.75


def shifted_hamiltonian(padded, potential, energy):
    axis_rows = padded.ndim - 3
    axis_cols = padded.ndim - 2
    length = padded.shape[axis_rows] - 12
    width = padded.shape[axis_cols]
    wrapped = jnp.concatenate([padded[..., width - 6:, :], padded, padded[..., :6, :]], axis=axis_cols)

    def take(row_off, col_off):
        part = lax.slice_in_dim(wrapped, 6 + row_off, 6 + row_off + length, axis=axis_rows)
        return lax.slice_in_dim(part, 6 + col_off, 6 + col_off + width, axis=axis_cols)

    center = take(0, 0)
    summed = 3.0 * STENCIL[0] * center
    for offset in range(1, 7):
        beside_all = take(offset, 0) + take(-offset, 0) + take(0, offset) + take(0, -offset)
        beside_all = beside_all + jnp.roll(center, offset, -1) + jnp.roll(center, -offset, -1)
        summed = summed + STENCIL[offset] * beside_all
    return (-0.5 / (SPACING * SPACING)) * summed + (potential - energy) * center


def pad_rows(field):
    return jnp.pad(field, ((6, 6), (0, 0), (0, 0)))


def reference(orbitals, potential, trial_potential, eigenvalues, frequency):
    squared = frequency[0] * frequency[0]

    def solve_one(item):
        orbital, energy = item

        def shifted(field):
            return shifted_hamiltonian(pad_rows(field), potential, energy)

        def operator(field):
            return shifted(shifted(field)) + squared * field

        source = trial_potential * orbital
        solution = jnp.zeros_like(source)
        residual = source
        direction = source
        norm_now = jnp.sum(residual * residual)
        for step in range(ITERS):
            image = operator(direction)
            step_size = norm_now / jnp.sum(direction * image)
            solution = solution + step_size * direction
            residual = residual - step_size * image
            norm_next = jnp.sum(residual * residual)
            direction = residual + (norm_next / norm_now) * direction
            norm_now = norm_next
        response = -4.0 * orbital * shifted(solution)
        return solution, response

    solutions, responses = lax.map(solve_one, (orbitals, eigenvalues))
    return solutions, jnp.sum(responses, axis=0)
```

```python
import functools

import jax
import jax.numpy as jnp
import numpy as np
from jax import lax
from jax.experimental import pallas as pl
from jax.experimental.pallas import tpu as pltpu
from jax.sharding import PartitionSpec as P

STENCIL = (
    -5369.0 / 1800.0,
    12.0 / 7.0,
    -15.0 / 56.0,
    10.0 / 189.0,
    -1.0 / 112.0,
    2.0 / 1925.0,
    -1.0 / 16632.0,
)
SPACING = 0.75
REACH = len(STENCIL) - 1
COEFS = tuple(-0.5 / (SPACING * SPACING) * c for c in STENCIL)
STRIP = 8


def circulant(size):
    full = np.zeros((size, size), np.float64)
    for row in range(size):
        for k in range(1, REACH + 1):
            full[row, (row + k) % size] += COEFS[k]
            full[row, (row - k) % size] += COEFS[k]
    high = full.astype(jnp.bfloat16)
    low = (full - high.astype(np.float64)).astype(jnp.bfloat16)
    return high, low


def kernel(
    n, chunks,
    orb_hbm, pot_hbm, tri_hbm, eig, freq, cz_hbm, cy_hbm,
    sol_hbm, den_hbm,
    orb, pot, tri, src, img, two, res, dirn, fin, cz, cy,
    hup, hlo, sums, coef, part, got, last,
    ld_sem, mat_sem, out_sem,
    dn_s, dn_r, up_s, up_r, sum_s, sum_r, part_s, part_r, last_s, last_r,
):
    planes, ny, nz = src.shape
    wide = coef.shape[1]
    quarter = part.shape[2]
    g = lax.axis_index("grid")
    o = lax.axis_index("orb")
    below, above = lax.rem(g + n - 1, n), lax.rem(g + 1, n)
    has_low, has_up = g > 0, g < n - 1
    odd = lax.rem(g, 2)
    flip1 = o + 1 - 2 * lax.rem(o, 2)
    flip2 = lax.rem(o + 2, 4)
    first = (1 - odd) * flip1 + odd * flip2
    second = odd * flip1 + (1 - odd) * flip2
    both = 3 - o
    energy = eig[0]
    squared = freq[0] * freq[0]

    barrier = pltpu.get_barrier_semaphore()
    for j in range(1, n):
        pl.semaphore_signal(barrier, inc=1, device_id={"grid": lax.rem(g + j, n)})
    pl.semaphore_signal(barrier, inc=1, device_id={"orb": first})
    pl.semaphore_signal(barrier, inc=1, device_id={"orb": second})

    order = []
    for k in range(REACH):
        order += [k, planes - 1 - k]
    order += list(range(REACH, planes - REACH))

    def load(which, p):
        hbm, ref = ((orb_hbm, orb), (tri_hbm, tri))[which]
        return pltpu.make_async_copy(hbm.at[p], ref.at[p], ld_sem.at[which, p])

    for p in order:
        load(0, p).start()
        load(1, p).start()
    mats = [
        pltpu.make_async_copy(cz_hbm, cz, mat_sem.at[0]),
        pltpu.make_async_copy(cy_hbm, cy, mat_sem.at[1]),
        pltpu.make_async_copy(pot_hbm, pot, mat_sem.at[2]),
    ]
    for copy in mats:
        copy.start()

    fields = (src, img, res)

    def down(r, k):
        return pltpu.make_async_remote_copy(
            src_ref=fields[r].at[k], dst_ref=hup.at[r, k],
            send_sem=dn_s.at[r, k], recv_sem=dn_r.at[r, k],
            device_id={"grid": below}, device_id_type=pl.DeviceIdType.MESH)

    def up(r, k):
        return pltpu.make_async_remote_copy(
            src_ref=fields[r].at[planes - 1 - k], dst_ref=hlo.at[r, k],
            send_sem=up_s.at[r, k], recv_sem=up_r.at[r, k],
            device_id={"grid": above}, device_id_type=pl.DeviceIdType.MESH)

    def send(r, p):
        if p < REACH:
            @pl.when(has_low)
            def _():
                down(r, p).start()
        if p >= planes - REACH:
            @pl.when(has_up)
            def _():
                up(r, planes - 1 - p).start()

    def rows_of(s, count):
        return pl.ds(pl.multiple_of(s * count, count), count)

    def over(step, init, count=wide):
        return lax.fori_loop(0, ny // count, step, init)

    zero = jnp.zeros((wide, nz), jnp.float32)

    def upper_pairs(k):
        return [(p, COEFS[planes + k - p]) for p in range(planes - REACH + k, planes)]

    def lower_pairs(k):
        return [(p, COEFS[p + 1 + k]) for p in range(0, REACH - k)]

    def add_halo(acc, halo, pairs):
        def step(s, carry):
            rows = rows_of(s, wide)
            value = halo[rows, :]
            for p, c in pairs:
                acc[p, rows, :] = acc[p, rows, :] + c * value
            return carry

        over(step, 0)

    def arrive(r, k, acc, upper=None, lower=None):
        @pl.when(has_up)
        def _():
            down(r, k).wait_recv()
            add_halo(acc, hup.at[r, k], upper_pairs(k))

        @pl.when(has_low)
        def _():
            up(r, k).wait_recv()
            add_halo(acc, hlo.at[r, k], lower_pairs(k))

    def square_of(ref, p, total):
        def step(s, carry):
            value = ref[p, rows_of(s, wide), :]
            return carry + value * value

        return over(step, total)

    def interior(value, out):
        def plane(p, carry):
            whole = value[p]
            high = whole.astype(jnp.bfloat16)
            low = (whole - high.astype(jnp.float32)).astype(jnp.bfloat16)
            along_z = jnp.dot(
                jnp.concatenate([high, low, high], axis=1), cz[...],
                preferred_element_type=jnp.float32)
            along_y = jnp.dot(
                cy[...], jnp.concatenate([high, low, high], axis=0),
                preferred_element_type=jnp.float32)
            out[p] = along_z + along_y
            return carry

        lax.fori_loop(0, planes, plane, 0)

        def strip(s, carry):
            rows = rows_of(s, STRIP)
            parts = [value[q, rows, :] for q in range(planes)]
            for p in range(planes):
                total = out[p, rows, :] + (pot[p, rows, :] + (3.0 * COEFS[0] - energy)) * parts[p]
                for k in range(1, REACH + 1):
                    near = [parts[q] for q in (p - k, p + k) if 0 <= q < planes]
                    if near:
                        total = total + COEFS[k] * (near[0] + near[1] if len(near) == 2 else near[0])
                out[p, rows, :] = total
            return carry

        over(strip, 0, STRIP)

    def fold(total):
        total = functools.reduce(
            lambda a, b: a + b, [total[i:i + 8] for i in range(0, wide, 8)])
        return functools.reduce(
            lambda a, b: a + b, [total[:, i:i + 128] for i in range(0, nz, 128)])

    def exchange(r, j, slot):
        return pltpu.make_async_remote_copy(
            src_ref=sums.at[r, slot], dst_ref=sums.at[r, slot],
            send_sem=sum_s.at[r, j], recv_sem=sum_r.at[r, j],
            device_id={"grid": lax.rem(g + j, n)}, device_id_type=pl.DeviceIdType.MESH)

    def post(r, *totals):
        for i, total in enumerate(totals):
            sums[r, g, i] = fold(total)
        for i in range(len(totals), sums.shape[2]):
            sums[r, g, i] = jnp.zeros(sums.shape[3:], jnp.float32)
        for j in range(1, n):
            exchange(r, j, g).start()

    def collect(r, i):
        total = sums[r, 0, i]
        for m in range(1, n):
            total = total + sums[r, m, i]
        return jnp.sum(total, keepdims=True)

    def await_sums(r):
        for j in range(1, n):
            exchange(r, j, lax.rem(g + n - j, n)).wait_recv()

    def keep(i, value):
        coef[i] = jnp.broadcast_to(value, (wide, nz))

    pl.semaphore_wait(barrier, n + 1)
    total_src = zero
    for p in order:
        load(0, p).wait()
        load(1, p).wait()

        def step(s, carry, p=p):
            rows = rows_of(s, wide)
            value = orb[p, rows, :] * tri[p, rows, :]
            src[p, rows, :] = value
            return carry + value * value

        total_src = over(step, total_src)
        send(0, p)
    for copy in mats:
        copy.wait()

    interior(src, img)
    total_img = zero
    for p in range(REACH, planes - REACH):
        total_img = square_of(img, p, total_img)
    for k in range(REACH):
        arrive(0, k, img)
        for p in (REACH - 1 - k, planes - REACH + k):
            total_img = square_of(img, p, total_img)
            send(1, p)
    post(0, total_src, total_img)

    interior(img, two)
    for k in range(REACH - 1, 0, -1):
        arrive(1, k, two)
    await_sums(0)
    norm0 = collect(0, 0)
    step0 = norm0 / (collect(0, 1) + squared * norm0)
    keep(0, step0)
    arrive(1, 0, two)
    total_res = zero
    for p in order:
        def step(s, carry, p=p):
            rows = rows_of(s, wide)
            start = src[p, rows, :]
            value = start - coef[0] * (two[p, rows, :] + squared * start)
            res[p, rows, :] = value
            return carry + value * value

        total_res = over(step, total_res)
        send(2, p)
    post(1, total_res)

    interior(res, fin)
    await_sums(1)
    norm1 = collect(1, 0)
    keep(1, norm1 / norm0)

    def direct(p, total):
        def step(s, carry):
            rows = rows_of(s, wide)
            value = res[p, rows, :] + coef[1] * src[p, rows, :]
            dirn[p, rows, :] = value
            fin[p, rows, :] = fin[p, rows, :] + coef[1] * img[p, rows, :]
            return carry + value * value

        return over(step, total)

    total_dir = lax.fori_loop(0, planes, direct, zero)
    total_fin = zero
    for p in range(REACH, planes - REACH):
        total_fin = square_of(fin, p, total_fin)
    for k in range(REACH):
        arrive(2, k, fin)
        for p in (REACH - 1 - k, planes - REACH + k):
            total_fin = square_of(fin, p, total_fin)
    post(2, total_dir, total_fin)
    await_sums(2)
    keep(2, norm1 / (collect(2, 1) + squared * collect(2, 0)))

    span = planes // chunks
    quarters = (both, first, second, o)

    def respond(slot, c):
        base = quarters[slot] * quarter

        def plane(i, carry):
            p = c * span + i
            rows = pl.ds(pl.multiple_of(base, 8), quarter)
            part[slot, p] = (-4.0 * orb[p, rows, :]) * (
                coef[0, 0:1, :] * img[p, rows, :] + coef[2, 0:1, :] * fin[p, rows, :])
            return carry

        lax.fori_loop(0, span, plane, 0)

    def hand(slot, c):
        some = pl.ds(c * span, span)
        return pltpu.make_async_remote_copy(
            src_ref=part.at[slot, some], dst_ref=got.at[slot, some],
            send_sem=part_s.at[slot, c], recv_sem=part_r.at[slot, c],
            device_id={"orb": first}, device_id_type=pl.DeviceIdType.MESH)

    def hand_last(c):
        some = pl.ds(c * span, span)
        return pltpu.make_async_remote_copy(
            src_ref=part.at[2, some], dst_ref=last.at[some],
            send_sem=last_s.at[c], recv_sem=last_r.at[c],
            device_id={"orb": second}, device_id_type=pl.DeviceIdType.MESH)

    for slot in (0, 1):
        for c in range(chunks):
            respond(slot, c)
            hand(slot, c).start()
    for slot in (2, 3):
        for c in range(chunks):
            respond(slot, c)

    for k in range(REACH):
        @pl.when(has_low)
        def _():
            down(0, k).wait_send()

        @pl.when(has_up)
        def _():
            up(0, k).wait_send()

    def solve(p, carry):
        def step(s, inner):
            rows = rows_of(s, wide)
            src[p, rows, :] = coef[0] * src[p, rows, :] + coef[2] * dirn[p, rows, :]
            return inner

        return over(step, carry)

    lax.fori_loop(0, planes, solve, 0)
    out_sol = pltpu.make_async_copy(src, sol_hbm, out_sem.at[0])
    out_sol.start()

    for c in range(chunks):
        hand(0, c).wait_recv()
        some = slice(c * span, (c + 1) * span)
        part[2, some] = part[2, some] + got[0, some]
        hand_last(c).start()
    for c in range(chunks):
        hand(1, c).wait_recv()
        hand_last(c).wait_recv()
        some = slice(c * span, (c + 1) * span)
        part[3, some] = part[3, some] + (got[1, some] + last[some])
    out_den = pltpu.make_async_copy(part.at[3], den_hbm, out_sem.at[1])
    out_den.start()

    for r in (1, 2):
        for k in range(REACH):
            @pl.when(has_low)
            def _():
                down(r, k).wait_send()

            @pl.when(has_up)
            def _():
                up(r, k).wait_send()
    for r in range(3):
        for j in range(1, n):
            exchange(r, j, g).wait_send()
    for c in range(chunks):
        hand(0, c).wait_send()
        hand(1, c).wait_send()
        hand_last(c).wait_send()
    out_sol.wait()
    out_den.wait()


def body(n, groups, orbitals, potential, trial_potential, eigenvalues, frequency):
    count, planes, ny, nz = orbitals.shape
    assert count == 1 and groups == 4 and planes >= 2 * REACH
    quarter = ny // groups
    wide = 32 if ny % 32 == 0 else 8
    chunks = 4 if planes % 4 == 0 else 1
    zh, zl = circulant(nz)
    yh, yl = circulant(ny)
    cz = jnp.asarray(np.concatenate([zh, zh, zl], axis=0))
    cy = jnp.asarray(np.concatenate([yh, yh, yl], axis=1))
    f32 = jnp.float32
    field = pltpu.VMEM((planes, ny, nz), f32)
    dma = pltpu.SemaphoreType.DMA
    anywhere = pl.BlockSpec(memory_space=pl.ANY)
    smem = pl.BlockSpec(memory_space=pltpu.SMEM)
    sol, den = pl.pallas_call(
        functools.partial(kernel, n, chunks),
        out_shape=(
            jax.ShapeDtypeStruct((planes, ny, nz), f32),
            jax.ShapeDtypeStruct((planes, quarter, nz), f32),
        ),
        in_specs=[anywhere] * 3 + [smem] * 2 + [anywhere] * 2,
        out_specs=(anywhere, anywhere),
        scratch_shapes=[field] * 9 + [
            pltpu.VMEM(cz.shape, cz.dtype),
            pltpu.VMEM(cy.shape, cy.dtype),
            pltpu.VMEM((3, REACH, ny, nz), f32),
            pltpu.VMEM((3, REACH, ny, nz), f32),
            pltpu.VMEM((3, n, 2, 8, 128), f32),
            pltpu.VMEM((3, wide, nz), f32),
            pltpu.VMEM((4, planes, quarter, nz), f32),
            pltpu.VMEM((2, planes, quarter, nz), f32),
            pltpu.VMEM((planes, quarter, nz), f32),
            dma((2, planes)), dma((3,)), dma((2,)),
            dma((3, REACH)), dma((3, REACH)), dma((3, REACH)), dma((3, REACH)),
            dma((3, n)), dma((3, n)),
            dma((2, chunks)), dma((2, chunks)), dma((chunks,)), dma((chunks,)),
        ],
        compiler_params=pltpu.CompilerParams(
            collective_id=0, has_side_effects=True, vmem_limit_bytes=60 * 2**20),
        name="sternheimer",
    )(
        orbitals.reshape(planes, ny, nz), potential, trial_potential,
        eigenvalues, frequency, cz, cy,
    )
    return sol.reshape(orbitals.shape), den


def solution(mesh):
    in_specs = (
        P("orb", "grid", None, None),
        P("grid", None, None),
        P("grid", None, None),
        P("orb"),
        P(),
    )
    out_specs = (P("orb", "grid", None, None), P("grid", "orb", None))
    call = functools.partial(body, mesh.shape["grid"], mesh.shape["orb"])
    return jax.shard_map(call, mesh=mesh, in_specs=in_specs, out_specs=out_specs, check_vma=False)
```

```python
import functools

import jax
import jax.numpy as jnp
import numpy as np
from jax import lax
from jax.experimental import pallas as pl
from jax.experimental.pallas import tpu as pltpu
from jax.sharding import PartitionSpec as P

STENCIL = (
    -5369.0 / 1800.0,
    12.0 / 7.0,
    -15.0 / 56.0,
    10.0 / 189.0,
    -1.0 / 112.0,
    2.0 / 1925.0,
    -1.0 / 16632.0,
)
SPACING = 0.75
REACH = len(STENCIL) - 1
COEFS = tuple(-0.5 / (SPACING * SPACING) * c for c in STENCIL)
STRIP = 8


def circulant(size):
    full = np.zeros((size, size), np.float64)
    for row in range(size):
        for k in range(1, REACH + 1):
            full[row, (row + k) % size] += COEFS[k]
            full[row, (row - k) % size] += COEFS[k]
    high = full.astype(jnp.bfloat16)
    low = (full - high.astype(np.float64)).astype(jnp.bfloat16)
    return high, low


def kernel(
    n,
    orb_hbm, pot_hbm, tri_hbm, eig, freq, cz_hbm, cy_hbm,
    sol_hbm, den_hbm,
    orb, pot, tri, src, img, two, res, dirn, fin, cz, cy,
    hup, hlo, sums, coef, part, got, last, ship, land, mix, dens,
    ld_sem, mat_sem, out_sem,
    dn_s, dn_r, up_s, up_r, sum_s, sum_r, part_s, part_r, last_s, last_r,
    ship_s, ship_r, mix_s, mix_r,
):
    planes, ny, nz = src.shape
    wide = coef.shape[1]
    quarter = part.shape[2]
    g = lax.axis_index("grid")
    o = lax.axis_index("orb")
    below, above = lax.rem(g + n - 1, n), lax.rem(g + 1, n)
    has_low, has_up = g > 0, g < n - 1
    odd = lax.rem(g, 2)
    flip1 = o + 1 - 2 * lax.rem(o, 2)
    flip2 = lax.rem(o + 2, 4)
    first = (1 - odd) * flip1 + odd * flip2
    second = odd * flip1 + (1 - odd) * flip2
    both = 3 - o
    energy = eig[0]
    squared = freq[0] * freq[0]

    barrier = pltpu.get_barrier_semaphore()
    for j in range(1, n):
        pl.semaphore_signal(barrier, inc=1, device_id={"grid": lax.rem(g + j, n)})
    pl.semaphore_signal(barrier, inc=1, device_id={"orb": first})
    pl.semaphore_signal(barrier, inc=1, device_id={"orb": second})
    pl.semaphore_signal(barrier, inc=1, device_id={"orb": both})

    order = []
    for k in range(REACH):
        order += [k, planes - 1 - k]
    order += list(range(REACH, planes - REACH))

    def load(which, p):
        hbm, ref = ((orb_hbm, orb), (tri_hbm, tri))[which]
        return pltpu.make_async_copy(hbm.at[p], ref.at[p], ld_sem.at[which, p])

    for p in order:
        load(0, p).start()
        load(1, p).start()
    mats = [
        pltpu.make_async_copy(cz_hbm, cz, mat_sem.at[0]),
        pltpu.make_async_copy(cy_hbm, cy, mat_sem.at[1]),
        pltpu.make_async_copy(pot_hbm, pot, mat_sem.at[2]),
    ]
    for copy in mats:
        copy.start()

    fields = (src, img, res)

    def down(r, k):
        return pltpu.make_async_remote_copy(
            src_ref=fields[r].at[k], dst_ref=hup.at[r, k],
            send_sem=dn_s.at[r, k], recv_sem=dn_r.at[r, k],
            device_id={"grid": below}, device_id_type=pl.DeviceIdType.MESH)

    def up(r, k):
        return pltpu.make_async_remote_copy(
            src_ref=fields[r].at[planes - 1 - k], dst_ref=hlo.at[r, k],
            send_sem=up_s.at[r, k], recv_sem=up_r.at[r, k],
            device_id={"grid": above}, device_id_type=pl.DeviceIdType.MESH)

    def send(r, p):
        if p < REACH:
            @pl.when(has_low)
            def _():
                down(r, p).start()
        if p >= planes - REACH:
            @pl.when(has_up)
            def _():
                up(r, planes - 1 - p).start()

    edge = planes // 4
    middle = range(edge, planes - edge)
    outer = list(range(edge)) + list(range(planes - edge, planes))
    quarters = (both, first, second, o)

    def rows_in(slot):
        return pl.ds(pl.multiple_of(quarters[slot] * quarter, 8), quarter)

    def ship_copy(field, slot, p):
        return pltpu.make_async_remote_copy(
            src_ref=ship.at[field, slot, p - edge], dst_ref=land.at[field, slot, p - edge],
            send_sem=ship_s.at[field, slot, p - edge], recv_sem=ship_r.at[field, slot, p - edge],
            device_id={"orb": quarters[slot]}, device_id_type=pl.DeviceIdType.MESH)

    def share(field, value, p):
        if p in middle:
            for slot in range(3):
                rows = rows_in(slot)
                ship[field, slot, p - edge] = orb[p, rows, :] * value[p, rows, :]
                ship_copy(field, slot, p).start()

    def rows_of(s, count):
        return pl.ds(pl.multiple_of(s * count, count), count)

    def over(step, init, count=wide):
        return lax.fori_loop(0, ny // count, step, init)

    zero = jnp.zeros((wide, nz), jnp.float32)

    def upper_pairs(k):
        return [(p, COEFS[planes + k - p]) for p in range(planes - REACH + k, planes)]

    def lower_pairs(k):
        return [(p, COEFS[p + 1 + k]) for p in range(0, REACH - k)]

    def add_halo(acc, halo, pairs):
        def step(s, carry):
            rows = rows_of(s, wide)
            value = halo[rows, :]
            for p, c in pairs:
                acc[p, rows, :] = acc[p, rows, :] + c * value
            return carry

        over(step, 0)

    def arrive(r, k, acc, upper=None, lower=None):
        @pl.when(has_up)
        def _():
            down(r, k).wait_recv()
            add_halo(acc, hup.at[r, k], upper_pairs(k))

        @pl.when(has_low)
        def _():
            up(r, k).wait_recv()
            add_halo(acc, hlo.at[r, k], lower_pairs(k))

    def square_of(ref, p, total):
        def step(s, carry):
            value = ref[p, rows_of(s, wide), :]
            return carry + value * value

        return over(step, total)

    def interior(value, out):
        def plane(p, carry):
            whole = value[p]
            high = whole.astype(jnp.bfloat16)
            low = (whole - high.astype(jnp.float32)).astype(jnp.bfloat16)
            along_z = jnp.dot(
                jnp.concatenate([high, low, high], axis=1), cz[...],
                preferred_element_type=jnp.float32)
            along_y = jnp.dot(
                cy[...], jnp.concatenate([high, low, high], axis=0),
                preferred_element_type=jnp.float32)
            out[p] = along_z + along_y
            return carry

        lax.fori_loop(0, planes, plane, 0)

        def strip(s, carry):
            rows = rows_of(s, STRIP)
            parts = [value[q, rows, :] for q in range(planes)]
            for p in range(planes):
                total = out[p, rows, :] + (pot[p, rows, :] + (3.0 * COEFS[0] - energy)) * parts[p]
                for k in range(1, REACH + 1):
                    near = [parts[q] for q in (p - k, p + k) if 0 <= q < planes]
                    if near:
                        total = total + COEFS[k] * (near[0] + near[1] if len(near) == 2 else near[0])
                out[p, rows, :] = total
            return carry

        over(strip, 0, STRIP)

    def fold(total):
        total = functools.reduce(
            lambda a, b: a + b, [total[i:i + 8] for i in range(0, wide, 8)])
        return functools.reduce(
            lambda a, b: a + b, [total[:, i:i + 128] for i in range(0, nz, 128)])

    def exchange(r, j, slot):
        return pltpu.make_async_remote_copy(
            src_ref=sums.at[r, slot], dst_ref=sums.at[r, slot],
            send_sem=sum_s.at[r, j], recv_sem=sum_r.at[r, j],
            device_id={"grid": lax.rem(g + j, n)}, device_id_type=pl.DeviceIdType.MESH)

    def post(r, *totals):
        for i, total in enumerate(totals):
            sums[r, g, i] = fold(total)
        if len(totals) == 1:
            sums[r, g, 1] = jnp.zeros(sums.shape[3:], jnp.float32)
        for j in range(1, n):
            exchange(r, j, g).start()

    def collect(r, i):
        total = sums[r, 0, i]
        for m in range(1, n):
            total = total + sums[r, m, i]
        return jnp.sum(total, keepdims=True)

    def await_sums(r):
        for j in range(1, n):
            exchange(r, j, lax.rem(g + n - j, n)).wait_recv()

    def keep(i, value):
        coef[i] = jnp.broadcast_to(value, (wide, nz))

    pl.semaphore_wait(barrier, n + 2)
    total_src = zero
    for p in order:
        load(0, p).wait()
        load(1, p).wait()

        def step(s, carry, p=p):
            rows = rows_of(s, wide)
            value = orb[p, rows, :] * tri[p, rows, :]
            src[p, rows, :] = value
            return carry + value * value

        total_src = over(step, total_src)
        send(0, p)
    for copy in mats:
        copy.wait()

    interior(src, img)
    total_img = zero
    for p in range(REACH, planes - REACH):
        total_img = square_of(img, p, total_img)
    held = []
    for k in range(REACH):
        arrive(0, k, img)
        for p in (REACH - 1 - k, planes - REACH + k):
            total_img = square_of(img, p, total_img)
            if k < REACH // 2:
                send(1, p)
            else:
                held.append(p)
    post(0, total_src, total_img)
    for p in held:
        send(1, p)
    for p in middle:
        share(0, img, p)

    interior(img, two)
    for k in range(REACH - 1, 0, -1):
        arrive(1, k, two)
    await_sums(0)
    norm0 = collect(0, 0)
    step0 = norm0 / (collect(0, 1) + squared * norm0)
    keep(0, step0)
    arrive(1, 0, two)
    total_res = zero
    for p in order:
        def step(s, carry, p=p):
            rows = rows_of(s, wide)
            start = src[p, rows, :]
            value = start - coef[0] * (two[p, rows, :] + squared * start)
            res[p, rows, :] = value
            return carry + value * value

        total_res = over(step, total_res)
        if p in order[:4]:
            send(2, p)
    post(1, total_res)
    for p in order[4:]:
        send(2, p)

    interior(res, fin)

    def direct(p, total):
        def step(s, carry):
            rows = rows_of(s, wide)
            value = res[p, rows, :] + coef[1] * src[p, rows, :]
            dirn[p, rows, :] = value
            return carry + value * value

        return over(step, total)

    def square_fin(p, total):
        def step(s, carry):
            rows = rows_of(s, wide)
            value = fin[p, rows, :] + coef[1] * img[p, rows, :]
            return carry + value * value

        return over(step, total)

    total_fin = zero
    done = list(range(REACH, planes - REACH))
    for p in done:
        share(1, fin, p)
    for k in range(REACH):
        if k == REACH - 2:
            await_sums(1)
            norm1 = collect(1, 0)
            ratio = norm1 / norm0
            keep(1, ratio)
            total_dir = lax.fori_loop(0, planes, direct, zero)
            for p in done:
                total_fin = square_fin(p, total_fin)
        arrive(2, k, fin)
        for p in (REACH - 1 - k, planes - REACH + k):
            done.append(p)
            share(1, fin, p)
            if k >= REACH - 2:
                total_fin = square_fin(p, total_fin)
    post(2, total_dir, total_fin)
    await_sums(2)
    step1 = norm1 / (collect(2, 1) + squared * collect(2, 0))
    keep(2, step1)

    mix[3, 0] = jnp.broadcast_to(-4.0 * (step0 + step1 * ratio), mix.shape[2:])
    mix[3, 1] = jnp.broadcast_to(-4.0 * step1, mix.shape[2:])

    def tell(slot):
        return pltpu.make_async_remote_copy(
            src_ref=mix.at[3], dst_ref=mix.at[slot],
            send_sem=mix_s.at[slot], recv_sem=mix_r.at[slot],
            device_id={"orb": quarters[slot]}, device_id_type=pl.DeviceIdType.MESH)

    for slot in range(3):
        tell(slot).start()

    def respond(slot, p):
        rows = rows_in(slot)
        return orb[p, rows, :] * (
            mix[3, 0, 0:1, :] * img[p, rows, :] + mix[3, 1, 0:1, :] * fin[p, rows, :])

    def hand(slot, c):
        return pltpu.make_async_remote_copy(
            src_ref=part.at[slot, c], dst_ref=got.at[slot, c],
            send_sem=part_s.at[slot, c], recv_sem=part_r.at[slot, c],
            device_id={"orb": first}, device_id_type=pl.DeviceIdType.MESH)

    def hand_last(c):
        return pltpu.make_async_remote_copy(
            src_ref=part.at[2, c], dst_ref=last.at[c],
            send_sem=last_s.at[c], recv_sem=last_r.at[c],
            device_id={"orb": second}, device_id_type=pl.DeviceIdType.MESH)

    for slot in (0, 1):
        for c, p in enumerate(outer):
            part[slot, c] = respond(slot, p)
            hand(slot, c).start()
    for c, p in enumerate(outer):
        part[2, c] = respond(2, p)
        dens[p] = respond(3, p)

    for k in range(REACH):
        @pl.when(has_low)
        def _():
            down(0, k).wait_send()

        @pl.when(has_up)
        def _():
            up(0, k).wait_send()

    def solve(p, carry):
        def step(s, inner):
            rows = rows_of(s, wide)
            src[p, rows, :] = coef[0] * src[p, rows, :] + coef[2] * dirn[p, rows, :]
            return inner

        return over(step, carry)

    lax.fori_loop(0, planes, solve, 0)
    out_sol = pltpu.make_async_copy(src, sol_hbm, out_sem.at[0])
    out_sol.start()

    for c in range(len(outer)):
        hand(0, c).wait_recv()
        part[2, c] = part[2, c] + got[0, c]
        hand_last(c).start()
    for slot in range(3):
        tell(slot).wait_recv()
    for p in middle:
        total = respond(3, p)
        for slot in range(3):
            for field in range(2):
                ship_copy(field, slot, p).wait_recv()
                total = total + mix[slot, field, 0:1, :] * land[field, slot, p - edge]
        dens[p] = total
    for c, p in enumerate(outer):
        hand(1, c).wait_recv()
        hand_last(c).wait_recv()
        dens[p] = dens[p] + (got[1, c] + last[c])
    out_den = pltpu.make_async_copy(dens, den_hbm, out_sem.at[1])
    out_den.start()

    for r in (1, 2):
        for k in range(REACH):
            @pl.when(has_low)
            def _():
                down(r, k).wait_send()

            @pl.when(has_up)
            def _():
                up(r, k).wait_send()
    for r in range(3):
        for j in range(1, n):
            exchange(r, j, g).wait_send()
    for slot in range(3):
        tell(slot).wait_send()
        for p in middle:
            ship_copy(0, slot, p).wait_send()
            ship_copy(1, slot, p).wait_send()
    for c in range(len(outer)):
        hand(0, c).wait_send()
        hand(1, c).wait_send()
        hand_last(c).wait_send()
    out_sol.wait()
    out_den.wait()


def body(n, groups, orbitals, potential, trial_potential, eigenvalues, frequency):
    count, planes, ny, nz = orbitals.shape
    assert count == 1 and groups == 4 and planes >= 2 * REACH
    quarter = ny // groups
    wide = 32 if ny % 32 == 0 else 8
    edge = planes // 4
    inner = planes - 2 * edge
    zh, zl = circulant(nz)
    yh, yl = circulant(ny)
    cz = jnp.asarray(np.concatenate([zh, zh, zl], axis=0))
    cy = jnp.asarray(np.concatenate([yh, yh, yl], axis=1))
    f32 = jnp.float32
    field = pltpu.VMEM((planes, ny, nz), f32)
    dma = pltpu.SemaphoreType.DMA
    anywhere = pl.BlockSpec(memory_space=pl.ANY)
    smem = pl.BlockSpec(memory_space=pltpu.SMEM)
    sol, den = pl.pallas_call(
        functools.partial(kernel, n),
        out_shape=(
            jax.ShapeDtypeStruct((planes, ny, nz), f32),
            jax.ShapeDtypeStruct((planes, quarter, nz), f32),
        ),
        in_specs=[anywhere] * 3 + [smem] * 2 + [anywhere] * 2,
        out_specs=(anywhere, anywhere),
        scratch_shapes=[field] * 9 + [
            pltpu.VMEM(cz.shape, cz.dtype),
            pltpu.VMEM(cy.shape, cy.dtype),
            pltpu.VMEM((3, REACH, ny, nz), f32),
            pltpu.VMEM((3, REACH, ny, nz), f32),
            pltpu.VMEM((3, n, 2, 8, 128), f32),
            pltpu.VMEM((3, wide, nz), f32),
            pltpu.VMEM((3, 2 * edge, quarter, nz), f32),
            pltpu.VMEM((2, 2 * edge, quarter, nz), f32),
            pltpu.VMEM((2 * edge, quarter, nz), f32),
            pltpu.VMEM((2, 3, inner, quarter, nz), f32),
            pltpu.VMEM((2, 3, inner, quarter, nz), f32),
            pltpu.VMEM((4, 2, 8, nz), f32),
            pltpu.VMEM((planes, quarter, nz), f32),
            dma((2, planes)), dma((3,)), dma((2,)),
            dma((3, REACH)), dma((3, REACH)), dma((3, REACH)), dma((3, REACH)),
            dma((3, n)), dma((3, n)),
            dma((2, 2 * edge)), dma((2, 2 * edge)), dma((2 * edge,)), dma((2 * edge,)),
            dma((2, 3, inner)), dma((2, 3, inner)), dma((3,)), dma((3,)),
        ],
        compiler_params=pltpu.CompilerParams(
            collective_id=0, has_side_effects=True, vmem_limit_bytes=60 * 2**20),
        name="sternheimer",
    )(
        orbitals.reshape(planes, ny, nz), potential, trial_potential,
        eigenvalues, frequency, cz, cy,
    )
    return sol.reshape(orbitals.shape), den


def solution(mesh):
    in_specs = (
        P("orb", "grid", None, None),
        P("grid", None, None),
        P("grid", None, None),
        P("orb"),
        P(),
    )
    out_specs = (P("orb", "grid", None, None), P("grid", "orb", None))
    call = functools.partial(body, mesh.shape["grid"], mesh.shape["orb"])
    return jax.shard_map(call, mesh=mesh, in_specs=in_specs, out_specs=out_specs, check_vma=False)
```

```python
import functools

import jax
import jax.numpy as jnp
from jax import lax
from jax.experimental import pallas as pl
from jax.experimental.pallas import tpu as pltpu
from jax.sharding import PartitionSpec as P

STENCIL = (
    -5369.0 / 1800.0,
    12.0 / 7.0,
    -15.0 / 56.0,
    10.0 / 189.0,
    -1.0 / 112.0,
    2.0 / 1925.0,
    -1.0 / 16632.0,
)
SPACING = 0.75
REACH = len(STENCIL) - 1
COEFS = tuple(-0.5 / (SPACING * SPACING) * c for c in STENCIL)
STRIP = 8


def circulant(ref, count):
    size = ref.shape[1]

    def step(s, carry):
        rows = pl.ds(pl.multiple_of(s * count, count), count)
        row = s * count + lax.broadcasted_iota(jnp.int32, (count, size), 0)
        apart = jnp.abs(row - lax.broadcasted_iota(jnp.int32, (count, size), 1))
        apart = jnp.minimum(apart, size - apart)
        full = jnp.zeros((count, size), jnp.float32)
        for k in range(1, REACH + 1):
            full = jnp.where(apart == k, COEFS[k], full)
        high = full.astype(jnp.bfloat16)
        ref[0, rows, :] = high
        ref[1, rows, :] = (full - high.astype(jnp.float32)).astype(jnp.bfloat16)
        return carry

    lax.fori_loop(0, size // count, step, 0)


def kernel(
    n,
    orb_hbm, pot_hbm, tri_hbm, eig_hbm, freq_hbm,
    src, dens,
    orb, pot, tri, img, two, res, dirn, fin, cz, cy,
    hup, hlo, sums, coef, part, got, last, ship, land, mix,
    eig, freq, wave_up, wave_down, ld_sem, mat_sem,
    dn_s, dn_r, up_s, up_r, sum_s, sum_r, part_s, part_r, last_s, last_r,
    ship_s, ship_r, mix_s, mix_r,
):
    planes, ny, nz = src.shape
    wide = coef.shape[1]
    quarter = part.shape[2]
    g = lax.axis_index("grid")
    o = lax.axis_index("orb")
    below, above = lax.rem(g + n - 1, n), lax.rem(g + 1, n)
    has_low, has_up = g > 0, g < n - 1
    odd = lax.rem(g, 2)
    flip1 = o + 1 - 2 * lax.rem(o, 2)
    flip2 = lax.rem(o + 2, 4)
    first = (1 - odd) * flip1 + odd * flip2
    second = odd * flip1 + (1 - odd) * flip2
    both = 3 - o

    barrier = pltpu.get_barrier_semaphore()
    @pl.when(has_low)
    def _():
        pl.semaphore_signal(barrier, inc=1, device_id={"grid": below})

    @pl.when(has_up)
    def _():
        pl.semaphore_signal(barrier, inc=1, device_id={"grid": above})

    pl.semaphore_signal(barrier, inc=1, device_id={"orb": first})
    pl.semaphore_signal(barrier, inc=1, device_id={"orb": second})
    pl.semaphore_signal(barrier, inc=1, device_id={"orb": both})

    order = []
    for k in range(REACH):
        order += [k, planes - 1 - k]
    order += list(range(REACH, planes - REACH))

    def load(which, p):
        hbm, ref = ((orb_hbm, orb), (tri_hbm, tri))[which]
        return pltpu.make_async_copy(hbm.at[p], ref.at[p], ld_sem.at[which, p])

    for p in order:
        load(0, p).start()
        load(1, p).start()
    mats = [
        pltpu.make_async_copy(pot_hbm, pot, mat_sem.at[0]),
        pltpu.make_async_copy(eig_hbm, eig, mat_sem.at[1]),
        pltpu.make_async_copy(freq_hbm, freq, mat_sem.at[2]),
    ]
    for copy in mats:
        copy.start()

    fields = (src, img, res)

    def down(r, k):
        return pltpu.make_async_remote_copy(
            src_ref=fields[r].at[k], dst_ref=hup.at[r, k],
            send_sem=dn_s.at[r, k], recv_sem=dn_r.at[r, k],
            device_id={"grid": below}, device_id_type=pl.DeviceIdType.MESH)

    def up(r, k):
        return pltpu.make_async_remote_copy(
            src_ref=fields[r].at[planes - 1 - k], dst_ref=hlo.at[r, k],
            send_sem=up_s.at[r, k], recv_sem=up_r.at[r, k],
            device_id={"grid": above}, device_id_type=pl.DeviceIdType.MESH)

    def send(r, p):
        if p < REACH:
            @pl.when(has_low)
            def _():
                down(r, p).start()
        if p >= planes - REACH:
            @pl.when(has_up)
            def _():
                up(r, planes - 1 - p).start()

    edge = planes // 4
    middle = range(edge, planes - edge)
    outer = list(range(edge)) + list(range(planes - edge, planes))
    quarters = (both, first, second, o)

    def rows_in(slot):
        return pl.ds(pl.multiple_of(quarters[slot] * quarter, 8), quarter)

    def ship_copy(field, slot, p):
        return pltpu.make_async_remote_copy(
            src_ref=ship.at[field, slot, p - edge], dst_ref=land.at[field, slot, p - edge],
            send_sem=ship_s.at[field, slot, p - edge], recv_sem=ship_r.at[field, slot, p - edge],
            device_id={"orb": quarters[slot]}, device_id_type=pl.DeviceIdType.MESH)

    def share(field, value, p):
        if p in middle:
            for slot in range(3):
                rows = rows_in(slot)
                ship[field, slot, p - edge] = orb[p, rows, :] * value[p, rows, :]
                ship_copy(field, slot, p).start()

    def rows_of(s, count):
        return pl.ds(pl.multiple_of(s * count, count), count)

    def over(step, init, count=wide):
        return lax.fori_loop(0, ny // count, step, init)

    zero = jnp.zeros((wide, nz), jnp.float32)

    def upper_pairs(k):
        return [(p, COEFS[planes + k - p]) for p in range(planes - REACH + k, planes)]

    def lower_pairs(k):
        return [(p, COEFS[p + 1 + k]) for p in range(0, REACH - k)]

    def add_halo(acc, halo, pairs):
        def step(s, carry):
            rows = rows_of(s, wide)
            value = halo[rows, :]
            for p, c in pairs:
                acc[p, rows, :] = acc[p, rows, :] + c * value
            return carry

        over(step, 0)

    def arrive(r, k, acc, upper=None, lower=None):
        @pl.when(has_up)
        def _():
            down(r, k).wait_recv()
            add_halo(acc, hup.at[r, k], upper_pairs(k))

        @pl.when(has_low)
        def _():
            up(r, k).wait_recv()
            add_halo(acc, hlo.at[r, k], lower_pairs(k))

    def square_of(ref, p, total):
        def step(s, carry):
            value = ref[p, rows_of(s, wide), :]
            return carry + value * value

        return over(step, total)

    def interior(value, out):
        def plane(p, carry):
            whole = value[p]
            high = whole.astype(jnp.bfloat16)
            low = (whole - high.astype(jnp.float32)).astype(jnp.bfloat16)
            product = functools.partial(jnp.dot, preferred_element_type=jnp.float32)
            along_z = product(high, cz[0]) + product(low, cz[0]) + product(high, cz[1])
            along_y = product(cy[0], high) + product(cy[0], low) + product(cy[1], high)
            out[p] = along_z + along_y
            return carry

        lax.fori_loop(0, planes, plane, 0)

        def strip(s, carry):
            rows = rows_of(s, STRIP)
            parts = [value[q, rows, :] for q in range(planes)]
            for p in range(planes):
                total = out[p, rows, :] + (pot[p, rows, :] + (3.0 * COEFS[0] - energy)) * parts[p]
                for k in range(1, REACH + 1):
                    near = [parts[q] for q in (p - k, p + k) if 0 <= q < planes]
                    if near:
                        total = total + COEFS[k] * (near[0] + near[1] if len(near) == 2 else near[0])
                out[p, rows, :] = total
            return carry

        over(strip, 0, STRIP)

    def fold(total):
        total = functools.reduce(
            lambda a, b: a + b, [total[i:i + 8] for i in range(0, wide, 8)])
        return functools.reduce(
            lambda a, b: a + b, [total[:, i:i + 128] for i in range(0, nz, 128)])

    def exchange(r, j, slot):
        return pltpu.make_async_remote_copy(
            src_ref=sums.at[r, slot], dst_ref=sums.at[r, slot],
            send_sem=sum_s.at[r, j], recv_sem=sum_r.at[r, j],
            device_id={"grid": lax.rem(g + j, n)}, device_id_type=pl.DeviceIdType.MESH)

    def post(r, *totals):
        for i, total in enumerate(totals):
            sums[r, g, i] = fold(total)
        if len(totals) == 1:
            sums[r, g, 1] = jnp.zeros(sums.shape[3:], jnp.float32)
        for j in range(1, n):
            exchange(r, j, g).start()

    def collect(r, i):
        total = sums[r, 0, i]
        for m in range(1, n):
            total = total + sums[r, m, i]
        return jnp.sum(total, keepdims=True)

    def await_sums(r):
        for j in range(1, n):
            exchange(r, j, lax.rem(g + n - j, n)).wait_recv()

    def keep(i, value):
        coef[i] = jnp.broadcast_to(value, (wide, nz))

    pl.semaphore_wait(barrier, 3 + jnp.minimum(g, 1) + jnp.minimum(n - 1 - g, 1))
    total_src = zero
    for p in order:
        load(0, p).wait()
        load(1, p).wait()

        def step(s, carry, p=p):
            rows = rows_of(s, wide)
            value = orb[p, rows, :] * tri[p, rows, :]
            src[p, rows, :] = value
            return carry + value * value

        total_src = over(step, total_src)
        send(0, p)
    for copy in mats:
        copy.wait()
    energy = eig[0]
    squared = freq[0] * freq[0]

    circulant(cz, 32)
    circulant(cy, 32)
    def pass_on(wave, has_from, has_to, to):
        @pl.when(has_from)
        def _():
            pl.semaphore_wait(wave, 1)

        @pl.when(has_to)
        def _():
            pl.semaphore_signal(wave, inc=1, device_id={"grid": to})

    interior(src, img)
    pass_on(wave_up, has_low, has_up, above)
    pass_on(wave_down, has_up, has_low, below)

    total_img = zero
    for p in range(REACH, planes - REACH):
        total_img = square_of(img, p, total_img)
    held = []
    for k in range(REACH):
        arrive(0, k, img)
        for p in (REACH - 1 - k, planes - REACH + k):
            total_img = square_of(img, p, total_img)
            if k < REACH // 2:
                send(1, p)
            else:
                held.append(p)
    post(0, total_src, total_img)
    for p in held:
        send(1, p)
    for p in middle:
        share(0, img, p)

    interior(img, two)
    for k in range(REACH - 1, 0, -1):
        arrive(1, k, two)
    await_sums(0)
    norm0 = collect(0, 0)
    step0 = norm0 / (collect(0, 1) + squared * norm0)
    keep(0, step0)
    @pl.when(has_up)
    def _():
        down(1, 0).wait_recv()

    @pl.when(has_low)
    def _():
        up(1, 0).wait_recv()

    total_res = zero
    for p in order:
        if p < REACH:
            @pl.when(has_low)
            def _():
                add_halo(two, hlo.at[1, 0], [(p, COEFS[p + 1])])

        if p >= planes - REACH:
            @pl.when(has_up)
            def _():
                add_halo(two, hup.at[1, 0], [(p, COEFS[planes - p])])

        def step(s, carry, p=p):
            rows = rows_of(s, wide)
            start = src[p, rows, :]
            value = start - coef[0] * (two[p, rows, :] + squared * start)
            res[p, rows, :] = value
            return carry + value * value

        total_res = over(step, total_res)
        if p in order[:4]:
            send(2, p)
    post(1, total_res)
    for p in order[4:]:
        send(2, p)

    interior(res, fin)

    def direct(p, total):
        def step(s, carry):
            rows = rows_of(s, wide)
            value = res[p, rows, :] + coef[1] * src[p, rows, :]
            dirn[p, rows, :] = value
            return carry + value * value

        return over(step, total)

    def square_fin(p, total):
        def step(s, carry):
            rows = rows_of(s, wide)
            value = fin[p, rows, :] + coef[1] * img[p, rows, :]
            return carry + value * value

        return over(step, total)

    total_fin = zero
    done = list(range(REACH, planes - REACH))
    for p in done:
        share(1, fin, p)
    for k in range(REACH):
        if k == REACH - 2:
            await_sums(1)
            norm1 = collect(1, 0)
            ratio = norm1 / norm0
            keep(1, ratio)
            total_dir = lax.fori_loop(0, planes, direct, zero)
            for p in done:
                total_fin = square_fin(p, total_fin)
        arrive(2, k, fin)
        for p in (REACH - 1 - k, planes - REACH + k):
            done.append(p)
            share(1, fin, p)
            if k >= REACH - 2:
                total_fin = square_fin(p, total_fin)
    post(2, total_dir, total_fin)
    await_sums(2)
    step1 = norm1 / (collect(2, 1) + squared * collect(2, 0))
    keep(2, step1)

    mix[3, 0] = jnp.broadcast_to(-4.0 * (step0 + step1 * ratio), mix.shape[2:])
    mix[3, 1] = jnp.broadcast_to(-4.0 * step1, mix.shape[2:])

    def tell(slot):
        return pltpu.make_async_remote_copy(
            src_ref=mix.at[3], dst_ref=mix.at[slot],
            send_sem=mix_s.at[slot], recv_sem=mix_r.at[slot],
            device_id={"orb": quarters[slot]}, device_id_type=pl.DeviceIdType.MESH)

    for slot in range(3):
        tell(slot).start()

    def respond(slot, p):
        rows = rows_in(slot)
        return orb[p, rows, :] * (
            mix[3, 0, 0:1, :] * img[p, rows, :] + mix[3, 1, 0:1, :] * fin[p, rows, :])

    def hand(slot, c):
        return pltpu.make_async_remote_copy(
            src_ref=part.at[slot, c], dst_ref=got.at[slot, c],
            send_sem=part_s.at[slot, c], recv_sem=part_r.at[slot, c],
            device_id={"orb": first}, device_id_type=pl.DeviceIdType.MESH)

    def hand_last(c):
        return pltpu.make_async_remote_copy(
            src_ref=part.at[2, c], dst_ref=last.at[c],
            send_sem=last_s.at[c], recv_sem=last_r.at[c],
            device_id={"orb": second}, device_id_type=pl.DeviceIdType.MESH)

    for slot in (0, 1):
        for c, p in enumerate(outer):
            part[slot, c] = respond(slot, p)
            hand(slot, c).start()
    for c, p in enumerate(outer):
        part[2, c] = respond(2, p)
        dens[p] = respond(3, p)

    for k in range(REACH):
        @pl.when(has_low)
        def _():
            down(0, k).wait_send()

        @pl.when(has_up)
        def _():
            up(0, k).wait_send()

    def solve(p, carry):
        def step(s, inner):
            rows = rows_of(s, wide)
            src[p, rows, :] = coef[0] * src[p, rows, :] + coef[2] * dirn[p, rows, :]
            return inner

        return over(step, carry)

    lax.fori_loop(0, planes, solve, 0)

    for c in range(len(outer)):
        hand(0, c).wait_recv()
        part[2, c] = part[2, c] + got[0, c]
        hand_last(c).start()
    for slot in range(3):
        tell(slot).wait_recv()
    for p in middle:
        total = respond(3, p)
        for slot in range(3):
            for field in range(2):
                ship_copy(field, slot, p).wait_recv()
                total = total + mix[slot, field, 0:1, :] * land[field, slot, p - edge]
        dens[p] = total
    for c, p in enumerate(outer):
        hand(1, c).wait_recv()
        hand_last(c).wait_recv()
        dens[p] = dens[p] + (got[1, c] + last[c])

    for r in (1, 2):
        for k in range(REACH):
            @pl.when(has_low)
            def _():
                down(r, k).wait_send()

            @pl.when(has_up)
            def _():
                up(r, k).wait_send()
    for r in range(3):
        for j in range(1, n):
            exchange(r, j, g).wait_send()
    for slot in range(3):
        tell(slot).wait_send()
        for p in middle:
            ship_copy(0, slot, p).wait_send()
            ship_copy(1, slot, p).wait_send()
    for c in range(len(outer)):
        hand(0, c).wait_send()
        hand(1, c).wait_send()
        hand_last(c).wait_send()


def write_out(sol, den, sol_hbm, den_hbm, sem):
    copies = [
        pltpu.make_async_copy(sol, sol_hbm, sem.at[0]),
        pltpu.make_async_copy(den, den_hbm, sem.at[1]),
    ]
    for copy in copies:
        copy.start()
    for copy in copies:
        copy.wait()


def body(n, groups, orbitals, potential, trial_potential, eigenvalues, frequency):
    count, planes, ny, nz = orbitals.shape
    assert count == 1 and groups == 4 and planes >= 2 * REACH
    assert ny % 32 == 0 and nz % 128 == 0 and min(ny, nz) > 2 * REACH
    quarter = ny // groups
    wide = 32
    edge = planes // 4
    inner = planes - 2 * edge
    f32 = jnp.float32
    field = pltpu.VMEM((planes, ny, nz), f32)
    dma = pltpu.SemaphoreType.DMA
    anywhere = pl.BlockSpec(memory_space=pl.ANY)
    hbm = pl.BlockSpec(memory_space=pltpu.HBM)
    vmem = pl.BlockSpec(memory_space=pltpu.VMEM)
    sol, den = pl.pallas_call(
        functools.partial(kernel, n),
        out_shape=(
            pltpu.VMEM((planes, ny, nz), f32),
            pltpu.VMEM((planes, quarter, nz), f32),
        ),
        in_specs=[hbm] * 5,
        out_specs=(vmem, vmem),
        scratch_shapes=[field] * 8 + [
            pltpu.VMEM((2, nz, nz), jnp.bfloat16),
            pltpu.VMEM((2, ny, ny), jnp.bfloat16),
            pltpu.VMEM((3, REACH, ny, nz), f32),
            pltpu.VMEM((3, REACH, ny, nz), f32),
            pltpu.VMEM((3, n, 2, 8, 128), f32),
            pltpu.VMEM((3, wide, nz), f32),
            pltpu.VMEM((3, 2 * edge, quarter, nz), f32),
            pltpu.VMEM((2, 2 * edge, quarter, nz), f32),
            pltpu.VMEM((2 * edge, quarter, nz), f32),
            pltpu.VMEM((2, 3, inner, quarter, nz), f32),
            pltpu.VMEM((2, 3, inner, quarter, nz), f32),
            pltpu.VMEM((4, 2, 8, nz), f32),
            pltpu.SMEM((1,), f32), pltpu.SMEM((1,), f32),
            pltpu.SemaphoreType.REGULAR, pltpu.SemaphoreType.REGULAR,
            dma((2, planes)), dma((3,)),
            dma((3, REACH)), dma((3, REACH)), dma((3, REACH)), dma((3, REACH)),
            dma((3, n)), dma((3, n)),
            dma((2, 2 * edge)), dma((2, 2 * edge)), dma((2 * edge,)), dma((2 * edge,)),
            dma((2, 3, inner)), dma((2, 3, inner)), dma((3,)), dma((3,)),
        ],
        compiler_params=pltpu.CompilerParams(
            collective_id=0, has_side_effects=True, vmem_limit_bytes=50 * 2**20),
        name="sternheimer",
    )(
        orbitals.reshape(planes, ny, nz), potential, trial_potential,
        eigenvalues, frequency,
    )
    sol, den = pl.pallas_call(
        write_out,
        out_shape=(jax.ShapeDtypeStruct(sol.shape, f32), jax.ShapeDtypeStruct(den.shape, f32)),
        in_specs=[vmem] * 2,
        out_specs=(anywhere, anywhere),
        scratch_shapes=[dma((2,))],
        compiler_params=pltpu.CompilerParams(vmem_limit_bytes=2**20),
        name="write_out",
    )(sol, den)
    return sol.reshape(orbitals.shape), den


def solution(mesh):
    in_specs = (
        P("orb", "grid", None, None),
        P("grid", None, None),
        P("grid", None, None),
        P("orb"),
        P(),
    )
    out_specs = (P("orb", "grid", None, None), P("grid", "orb", None))
    call = functools.partial(body, mesh.shape["grid"], mesh.shape["orb"])
    return jax.shard_map(call, mesh=mesh, in_specs=in_specs, out_specs=out_specs, check_vma=False)
```

```python
import functools

import jax
import jax.numpy as jnp
from jax import lax
from jax.experimental import pallas as pl
from jax.experimental.pallas import tpu as pltpu
from jax.sharding import PartitionSpec as P

STENCIL = (
    -5369.0 / 1800.0,
    12.0 / 7.0,
    -15.0 / 56.0,
    10.0 / 189.0,
    -1.0 / 112.0,
    2.0 / 1925.0,
    -1.0 / 16632.0,
)
SPACING = 0.75
REACH = len(STENCIL) - 1
COEFS = tuple(-0.5 / (SPACING * SPACING) * c for c in STENCIL)
STRIP = 8


def circulant(ref, count):
    size = ref.shape[1]

    def step(s, carry):
        rows = pl.ds(pl.multiple_of(s * count, count), count)
        row = s * count + lax.broadcasted_iota(jnp.int32, (count, size), 0)
        apart = jnp.abs(row - lax.broadcasted_iota(jnp.int32, (count, size), 1))
        apart = jnp.minimum(apart, size - apart)
        full = jnp.zeros((count, size), jnp.float32)
        for k in range(1, REACH + 1):
            full = jnp.where(apart == k, COEFS[k], full)
        high = full.astype(jnp.bfloat16)
        ref[0, rows, :] = high
        ref[1, rows, :] = (full - high.astype(jnp.float32)).astype(jnp.bfloat16)
        return carry

    lax.fori_loop(0, size // count, step, 0)


def kernel(
    n,
    orb_hbm, pot_hbm, tri_hbm, eig_hbm, freq_hbm,
    src, dens,
    orb, pot, tri, img, two, res, dirn, fin, cz, cy,
    hup, hlo, sums, coef, part, got, last, ship, land, mix,
    eig, freq, wave_up, wave_down, ld_sem, mat_sem,
    dn_s, dn_r, up_s, up_r, sum_s, sum_r, part_s, part_r, last_s, last_r,
    ship_s, ship_r, mix_s, mix_r,
):
    planes, ny, nz = src.shape
    wide = coef.shape[1]
    quarter = part.shape[2]
    g = lax.axis_index("grid")
    o = lax.axis_index("orb")
    below, above = lax.rem(g + n - 1, n), lax.rem(g + 1, n)
    has_low, has_up = g > 0, g < n - 1
    odd = lax.rem(g, 2)
    flip1 = o + 1 - 2 * lax.rem(o, 2)
    flip2 = lax.rem(o + 2, 4)
    first = (1 - odd) * flip1 + odd * flip2
    second = odd * flip1 + (1 - odd) * flip2
    both = 3 - o

    barrier = pltpu.get_barrier_semaphore()
    @pl.when(has_low)
    def _():
        pl.semaphore_signal(barrier, inc=1, device_id={"grid": below})

    @pl.when(has_up)
    def _():
        pl.semaphore_signal(barrier, inc=1, device_id={"grid": above})

    pl.semaphore_signal(barrier, inc=1, device_id={"orb": first})
    pl.semaphore_signal(barrier, inc=1, device_id={"orb": second})
    pl.semaphore_signal(barrier, inc=1, device_id={"orb": both})

    order = []
    for k in range(REACH):
        order += [k, planes - 1 - k]
    order += list(range(REACH, planes - REACH))

    def load(which, p):
        hbm, ref = ((orb_hbm, orb), (tri_hbm, tri))[which]
        return pltpu.make_async_copy(hbm.at[p], ref.at[p], ld_sem.at[which, p])

    for p in order:
        load(0, p).start()
        load(1, p).start()
    mats = [
        pltpu.make_async_copy(pot_hbm, pot, mat_sem.at[0]),
        pltpu.make_async_copy(eig_hbm, eig, mat_sem.at[1]),
        pltpu.make_async_copy(freq_hbm, freq, mat_sem.at[2]),
    ]
    for copy in mats:
        copy.start()

    fields = (src, img, res)

    def down(r, k):
        return pltpu.make_async_remote_copy(
            src_ref=fields[r].at[k], dst_ref=hup.at[r, k],
            send_sem=dn_s.at[r, k], recv_sem=dn_r.at[r, k],
            device_id={"grid": below}, device_id_type=pl.DeviceIdType.MESH)

    def up(r, k):
        return pltpu.make_async_remote_copy(
            src_ref=fields[r].at[planes - 1 - k], dst_ref=hlo.at[r, k],
            send_sem=up_s.at[r, k], recv_sem=up_r.at[r, k],
            device_id={"grid": above}, device_id_type=pl.DeviceIdType.MESH)

    def send(r, p):
        if p < REACH:
            @pl.when(has_low)
            def _():
                down(r, p).start()
        if p >= planes - REACH:
            @pl.when(has_up)
            def _():
                up(r, planes - 1 - p).start()

    edge = planes // 6
    middle = range(edge, planes - edge)
    outer = list(range(edge)) + list(range(planes - edge, planes))
    quarters = (both, first, second, o)

    def rows_in(slot):
        return pl.ds(pl.multiple_of(quarters[slot] * quarter, 8), quarter)

    def ship_copy(field, slot, p):
        return pltpu.make_async_remote_copy(
            src_ref=ship.at[field, slot, p - edge], dst_ref=land.at[field, slot, p - edge],
            send_sem=ship_s.at[field, slot, p - edge], recv_sem=ship_r.at[field, slot, p - edge],
            device_id={"orb": quarters[slot]}, device_id_type=pl.DeviceIdType.MESH)

    def share(field, value, p):
        if p in middle:
            for slot in range(3):
                rows = rows_in(slot)
                ship[field, slot, p - edge] = orb[p, rows, :] * value[p, rows, :]
                ship_copy(field, slot, p).start()

    def rows_of(s, count):
        return pl.ds(pl.multiple_of(s * count, count), count)

    def over(step, init, count=wide):
        return lax.fori_loop(0, ny // count, step, init)

    zero = jnp.zeros((wide, nz), jnp.float32)

    def upper_pairs(k):
        return [(p, COEFS[planes + k - p]) for p in range(planes - REACH + k, planes)]

    def lower_pairs(k):
        return [(p, COEFS[p + 1 + k]) for p in range(0, REACH - k)]

    def add_halo(acc, halo, pairs):
        def step(s, carry):
            rows = rows_of(s, wide)
            value = halo[rows, :]
            for p, c in pairs:
                acc[p, rows, :] = acc[p, rows, :] + c * value
            return carry

        over(step, 0)

    def arrive(r, k, acc, upper=None, lower=None):
        @pl.when(has_up)
        def _():
            down(r, k).wait_recv()
            add_halo(acc, hup.at[r, k], upper_pairs(k))

        @pl.when(has_low)
        def _():
            up(r, k).wait_recv()
            add_halo(acc, hlo.at[r, k], lower_pairs(k))

    def square_of(ref, p, total):
        def step(s, carry):
            value = ref[p, rows_of(s, wide), :]
            return carry + value * value

        return over(step, total)

    def interior(value, out):
        def plane(p, carry):
            whole = value[p]
            high = whole.astype(jnp.bfloat16)
            low = (whole - high.astype(jnp.float32)).astype(jnp.bfloat16)
            product = functools.partial(jnp.dot, preferred_element_type=jnp.float32)
            along_z = product(high, cz[0]) + product(low, cz[0]) + product(high, cz[1])
            along_y = product(cy[0], high) + product(cy[0], low) + product(cy[1], high)
            out[p] = along_z + along_y
            return carry

        lax.fori_loop(0, planes, plane, 0)

        def strip(s, carry):
            rows = rows_of(s, STRIP)
            parts = [value[q, rows, :] for q in range(planes)]
            for p in range(planes):
                total = out[p, rows, :] + (pot[p, rows, :] + (3.0 * COEFS[0] - energy)) * parts[p]
                for k in range(1, REACH + 1):
                    near = [parts[q] for q in (p - k, p + k) if 0 <= q < planes]
                    if near:
                        total = total + COEFS[k] * (near[0] + near[1] if len(near) == 2 else near[0])
                out[p, rows, :] = total
            return carry

        over(strip, 0, STRIP)

    def fold(total):
        total = functools.reduce(
            lambda a, b: a + b, [total[i:i + 8] for i in range(0, wide, 8)])
        return functools.reduce(
            lambda a, b: a + b, [total[:, i:i + 128] for i in range(0, nz, 128)])

    def exchange(r, j, slot):
        return pltpu.make_async_remote_copy(
            src_ref=sums.at[r, slot], dst_ref=sums.at[r, slot],
            send_sem=sum_s.at[r, j], recv_sem=sum_r.at[r, j],
            device_id={"grid": lax.rem(g + j, n)}, device_id_type=pl.DeviceIdType.MESH)

    def post(r, *totals):
        for i, total in enumerate(totals):
            sums[r, g, i] = fold(total)
        if len(totals) == 1:
            sums[r, g, 1] = jnp.zeros(sums.shape[3:], jnp.float32)
        for j in range(1, n):
            exchange(r, j, g).start()

    def collect(r, i):
        total = sums[r, 0, i]
        for m in range(1, n):
            total = total + sums[r, m, i]
        return jnp.sum(total, keepdims=True)

    def await_sums(r):
        for j in range(1, n):
            exchange(r, j, lax.rem(g + n - j, n)).wait_recv()

    def keep(i, value):
        coef[i] = jnp.broadcast_to(value, (wide, nz))

    pl.semaphore_wait(barrier, 3 + jnp.minimum(g, 1) + jnp.minimum(n - 1 - g, 1))
    total_src = zero
    for p in order:
        load(0, p).wait()
        load(1, p).wait()

        def step(s, carry, p=p):
            rows = rows_of(s, wide)
            value = orb[p, rows, :] * tri[p, rows, :]
            src[p, rows, :] = value
            return carry + value * value

        total_src = over(step, total_src)
        send(0, p)
    for copy in mats:
        copy.wait()
    energy = eig[0]
    squared = freq[0] * freq[0]

    circulant(cz, 32)
    circulant(cy, 32)
    def pass_on(wave, has_from, has_to, to):
        @pl.when(has_from)
        def _():
            pl.semaphore_wait(wave, 1)

        @pl.when(has_to)
        def _():
            pl.semaphore_signal(wave, inc=1, device_id={"grid": to})

    interior(src, img)
    pass_on(wave_up, has_low, has_up, above)
    pass_on(wave_down, has_up, has_low, below)

    total_img = zero
    for p in range(REACH, planes - REACH):
        total_img = square_of(img, p, total_img)
    held = []
    for k in range(REACH):
        arrive(0, k, img)
        for p in (REACH - 1 - k, planes - REACH + k):
            total_img = square_of(img, p, total_img)
            if k < REACH // 2:
                send(1, p)
            else:
                held.append(p)
    post(0, total_src, total_img)
    for p in held:
        send(1, p)
    for p in middle:
        share(0, img, p)

    interior(img, two)
    for k in range(REACH - 1, 0, -1):
        arrive(1, k, two)
    await_sums(0)
    norm0 = collect(0, 0)
    step0 = norm0 / (collect(0, 1) + squared * norm0)
    keep(0, step0)
    @pl.when(has_up)
    def _():
        down(1, 0).wait_recv()

    @pl.when(has_low)
    def _():
        up(1, 0).wait_recv()

    total_res = zero
    for p in order:
        if p < REACH:
            @pl.when(has_low)
            def _():
                add_halo(two, hlo.at[1, 0], [(p, COEFS[p + 1])])

        if p >= planes - REACH:
            @pl.when(has_up)
            def _():
                add_halo(two, hup.at[1, 0], [(p, COEFS[planes - p])])

        def step(s, carry, p=p):
            rows = rows_of(s, wide)
            start = src[p, rows, :]
            value = start - coef[0] * (two[p, rows, :] + squared * start)
            res[p, rows, :] = value
            return carry + value * value

        total_res = over(step, total_res)
        if p in order[:4]:
            send(2, p)
    post(1, total_res)
    for p in order[4:]:
        send(2, p)

    interior(res, fin)

    def direct(p, total):
        def step(s, carry):
            rows = rows_of(s, wide)
            value = res[p, rows, :] + coef[1] * src[p, rows, :]
            dirn[p, rows, :] = value
            return carry + value * value

        return over(step, total)

    def square_fin(p, total):
        def step(s, carry):
            rows = rows_of(s, wide)
            value = fin[p, rows, :] + coef[1] * img[p, rows, :]
            return carry + value * value

        return over(step, total)

    total_fin = zero
    done = list(range(REACH, planes - REACH))
    for p in done:
        share(1, fin, p)
    for k in range(REACH):
        if k == REACH - 2:
            await_sums(1)
            norm1 = collect(1, 0)
            ratio = norm1 / norm0
            keep(1, ratio)
            total_dir = lax.fori_loop(0, planes, direct, zero)
            for p in done:
                total_fin = square_fin(p, total_fin)
        arrive(2, k, fin)
        for p in (REACH - 1 - k, planes - REACH + k):
            done.append(p)
            share(1, fin, p)
            if k >= REACH - 2:
                total_fin = square_fin(p, total_fin)
    post(2, total_dir, total_fin)
    await_sums(2)
    step1 = norm1 / (collect(2, 1) + squared * collect(2, 0))
    keep(2, step1)

    mix[3, 0] = jnp.broadcast_to(-4.0 * (step0 + step1 * ratio), mix.shape[2:])
    mix[3, 1] = jnp.broadcast_to(-4.0 * step1, mix.shape[2:])

    def tell(slot):
        return pltpu.make_async_remote_copy(
            src_ref=mix.at[3], dst_ref=mix.at[slot],
            send_sem=mix_s.at[slot], recv_sem=mix_r.at[slot],
            device_id={"orb": quarters[slot]}, device_id_type=pl.DeviceIdType.MESH)

    for slot in range(3):
        tell(slot).start()

    def respond(slot, p):
        rows = rows_in(slot)
        return orb[p, rows, :] * (
            mix[3, 0, 0:1, :] * img[p, rows, :] + mix[3, 1, 0:1, :] * fin[p, rows, :])

    def hand(slot, c):
        return pltpu.make_async_remote_copy(
            src_ref=part.at[slot, c], dst_ref=got.at[slot, c],
            send_sem=part_s.at[slot, c], recv_sem=part_r.at[slot, c],
            device_id={"orb": first}, device_id_type=pl.DeviceIdType.MESH)

    def hand_last(c):
        return pltpu.make_async_remote_copy(
            src_ref=part.at[2, c], dst_ref=last.at[c],
            send_sem=last_s.at[c], recv_sem=last_r.at[c],
            device_id={"orb": second}, device_id_type=pl.DeviceIdType.MESH)

    for slot in (0, 1):
        for c, p in enumerate(outer):
            part[slot, c] = respond(slot, p)
            hand(slot, c).start()
    for c, p in enumerate(outer):
        part[2, c] = respond(2, p)
        dens[p] = respond(3, p)

    for k in range(REACH):
        @pl.when(has_low)
        def _():
            down(0, k).wait_send()

        @pl.when(has_up)
        def _():
            up(0, k).wait_send()

    def solve(p, carry):
        def step(s, inner):
            rows = rows_of(s, wide)
            src[p, rows, :] = coef[0] * src[p, rows, :] + coef[2] * dirn[p, rows, :]
            return inner

        return over(step, carry)

    lax.fori_loop(0, planes, solve, 0)

    for c in range(len(outer)):
        hand(0, c).wait_recv()
        part[2, c] = part[2, c] + got[0, c]
        hand_last(c).start()
    for slot in range(3):
        tell(slot).wait_recv()
    for p in middle:
        total = respond(3, p)
        for slot in range(3):
            for field in range(2):
                ship_copy(field, slot, p).wait_recv()
                total = total + mix[slot, field, 0:1, :] * land[field, slot, p - edge]
        dens[p] = total
    for c, p in enumerate(outer):
        hand(1, c).wait_recv()
        hand_last(c).wait_recv()
        dens[p] = dens[p] + (got[1, c] + last[c])

    for r in (1, 2):
        for k in range(REACH):
            @pl.when(has_low)
            def _():
                down(r, k).wait_send()

            @pl.when(has_up)
            def _():
                up(r, k).wait_send()
    for r in range(3):
        for j in range(1, n):
            exchange(r, j, g).wait_send()
    for slot in range(3):
        tell(slot).wait_send()
        for p in middle:
            ship_copy(0, slot, p).wait_send()
            ship_copy(1, slot, p).wait_send()
    for c in range(len(outer)):
        hand(0, c).wait_send()
        hand(1, c).wait_send()
        hand_last(c).wait_send()


def write_out(sol, den, sol_hbm, den_hbm, sem):
    copies = [
        pltpu.make_async_copy(sol, sol_hbm, sem.at[0]),
        pltpu.make_async_copy(den, den_hbm, sem.at[1]),
    ]
    for copy in copies:
        copy.start()
    for copy in copies:
        copy.wait()


def body(n, groups, orbitals, potential, trial_potential, eigenvalues, frequency):
    count, planes, ny, nz = orbitals.shape
    assert count == 1 and groups == 4 and planes >= 2 * REACH
    assert ny % 32 == 0 and nz % 128 == 0 and min(ny, nz) > 2 * REACH
    quarter = ny // groups
    wide = 32
    edge = planes // 6
    inner = planes - 2 * edge
    f32 = jnp.float32
    field = pltpu.VMEM((planes, ny, nz), f32)
    dma = pltpu.SemaphoreType.DMA
    anywhere = pl.BlockSpec(memory_space=pl.ANY)
    hbm = pl.BlockSpec(memory_space=pltpu.HBM)
    vmem = pl.BlockSpec(memory_space=pltpu.VMEM)
    sol, den = pl.pallas_call(
        functools.partial(kernel, n),
        out_shape=(
            pltpu.VMEM((planes, ny, nz), f32),
            pltpu.VMEM((planes, quarter, nz), f32),
        ),
        in_specs=[hbm] * 5,
        out_specs=(vmem, vmem),
        scratch_shapes=[field] * 8 + [
            pltpu.VMEM((2, nz, nz), jnp.bfloat16),
            pltpu.VMEM((2, ny, ny), jnp.bfloat16),
            pltpu.VMEM((3, REACH, ny, nz), f32),
            pltpu.VMEM((3, REACH, ny, nz), f32),
            pltpu.VMEM((3, n, 2, 8, 128), f32),
            pltpu.VMEM((3, wide, nz), f32),
            pltpu.VMEM((3, 2 * edge, quarter, nz), f32),
            pltpu.VMEM((2, 2 * edge, quarter, nz), f32),
            pltpu.VMEM((2 * edge, quarter, nz), f32),
            pltpu.VMEM((2, 3, inner, quarter, nz), f32),
            pltpu.VMEM((2, 3, inner, quarter, nz), f32),
            pltpu.VMEM((4, 2, 8, nz), f32),
            pltpu.SMEM((1,), f32), pltpu.SMEM((1,), f32),
            pltpu.SemaphoreType.REGULAR, pltpu.SemaphoreType.REGULAR,
            dma((2, planes)), dma((3,)),
            dma((3, REACH)), dma((3, REACH)), dma((3, REACH)), dma((3, REACH)),
            dma((3, n)), dma((3, n)),
            dma((2, 2 * edge)), dma((2, 2 * edge)), dma((2 * edge,)), dma((2 * edge,)),
            dma((2, 3, inner)), dma((2, 3, inner)), dma((3,)), dma((3,)),
        ],
        compiler_params=pltpu.CompilerParams(
            collective_id=0, has_side_effects=True, vmem_limit_bytes=50 * 2**20),
        name="sternheimer",
    )(
        orbitals.reshape(planes, ny, nz), potential, trial_potential,
        eigenvalues, frequency,
    )
    sol, den = pl.pallas_call(
        write_out,
        out_shape=(jax.ShapeDtypeStruct(sol.shape, f32), jax.ShapeDtypeStruct(den.shape, f32)),
        in_specs=[vmem] * 2,
        out_specs=(anywhere, anywhere),
        scratch_shapes=[dma((2,))],
        compiler_params=pltpu.CompilerParams(vmem_limit_bytes=2**20),
        name="write_out",
    )(sol, den)
    return sol.reshape(orbitals.shape), den


def solution(mesh):
    in_specs = (
        P("orb", "grid", None, None),
        P("grid", None, None),
        P("grid", None, None),
        P("orb"),
        P(),
    )
    out_specs = (P("orb", "grid", None, None), P("grid", "orb", None))
    call = functools.partial(body, mesh.shape["grid"], mesh.shape["orb"])
    return jax.shard_map(call, mesh=mesh, in_specs=in_specs, out_specs=out_specs, check_vma=False)
```
